32 devices in a mesh: row: 8 (over y, x, core), col: 4 (over z).
Axes of the slice: x: 2, y: 2, z: 4, core: 2. Of those that a mesh axis runs over, the one named last changes fastest.
Arguments:
- sub_basis: bfloat16 [32, 768, 768], P(('row', 'col')), may hold values from -0.15625 to 0.15625
- coupling: bfloat16 [32, 2, 768, 768], P(('row', 'col')), may hold values from -0.15625 to 0.15625
- pair_live: int32 [32, 2], P(('row', 'col')), may hold values 0 or 1
- offsets: int32 [32], P(('row', 'col')), may hold values from 0 to 3328
- dual_in: float32 [4, 4096], P('col', 'row'), may hold values from -6 to 6
Outputs:
- dual_out: float32 [4, 4096], P('col', 'row')
The draws below stay inside these ranges and needn't reach their ends.
Inputs may be any that keep to these rules, and one draw needn't show every extreme that they name: `offsets`: each subdomain's window of 768 multipliers lies inside its block column's vector.
All inputs are finite; a program needn't handle non-finite values. No bound on the sum of `pair_live` on one device may be relied on, other than what follows from the above.
Results may differ from the reference program's by a relative error of at most 0.0085.
Values may be sent and summed in bfloat16 or wider, within the bound.
A program may use at most 64 MiB of HBM per device.

```python
import jax
import jax.numpy as jnp
from jax import lax

W = 768
K = 768
HOPS = 2
SLICE = 512
SUBS = 32
DUALS = 4096
N_ROW = 8
N_COL = 4


def place_ends(array, key, least, high):
    longest = array.shape.index(max(array.shape))
    spots = []
    for shift in (0, 1):
        where = [jax.random.randint(jax.random.fold_in(key, axis), (), 0, length) for axis, length in enumerate(array.shape)]
        where[longest] = (where[longest] + shift) % array.shape[longest]
        spots.append(tuple(where))
    return array.at[spots[0]].set(least).at[spots[1]].set(high)


def shard_levels(own_key, dims, split, smallest, top_value):
    loudness = 1.0
    for position, shards_of in split:
        draws = jax.random.uniform(jax.random.fold_in(jax.random.fold_in(own_key, 6), position), (shards_of,), jnp.float32, smallest / len(split), top_value / len(split))
        loudness = loudness * jnp.repeat(jnp.exp(draws), dims[position] // shards_of).reshape((-1,) + (1,) * (len(dims) - 1 - position))
    return loudness


def scatter_about(key, dims, spread, reach, shards=(), kind=jnp.bfloat16):
    array = jax.random.normal(key, dims, jnp.float32) * spread
    if len(shards) > 0:
        array = shard_levels(key, dims, shards, -0.22, 0.18) * array
    return jnp.clip(array, min=-reach, max=reach).astype(kind)


def setup_inputs(seed: int = 0) -> dict:
    key_list = jax.random.split(jax.random.key(seed), 6)
    return {
        "sub_basis": scatter_about(key_list[0], (SUBS, K, W), (2 * K) ** -0.5, 0.15625, ((0, 32),)),
        "coupling": scatter_about(key_list[1], (SUBS, HOPS, K, W), (2 * K) ** -0.5, 0.15625, ((0, 32),)),
        "pair_live": place_ends((jax.random.randint(key_list[2], (SUBS, HOPS), 0, 4) < 3).astype(jnp.int32), jax.random.fold_in(key_list[2], 1), 0, 1),
        "offsets": place_ends(jax.random.randint(key_list[3], (SUBS,), 0, DUALS - W + 1), jax.random.fold_in(key_list[3], 1), 0, DUALS - W).astype(jnp.int32),
        "dual_in": scatter_about(key_list[4], (N_COL, DUALS), 1.0, 6.0, ((0, 4), (1, 8)), jnp.float32),
    }


def form_blocks(sub_basis, coupling, pair_live):
    def single(items):
        basis_one, coupling_one, live_one = items
        made = jnp.einsum("kv,hkw->hvw", basis_one.astype(jnp.float32), coupling_one.astype(jnp.float32), precision=lax.Precision.HIGHEST)
        made = made.astype(jnp.bfloat16)
        return made * live_one[:, None, None].astype(jnp.bfloat16)
    return lax.map(single, (sub_basis, coupling, pair_live))


def apply_dual(column_vec, sub_basis, blocks, offsets):
    count = sub_basis.shape[0]
    columns = (jnp.arange(count, dtype=jnp.int32) % N_COL).astype(jnp.int32)

    def cut_window(column, first_index):
        return lax.dynamic_slice(column_vec, (column.astype(jnp.int32), first_index.astype(jnp.int32)), (1, W))[0]

    windows = jax.vmap(cut_window)(columns, offsets)
    grid = windows.reshape(N_ROW, N_COL, W)
    leading = jnp.stack([jnp.roll(grid, -(slot_index + 1), axis=1).reshape(count, W) for slot_index in range(HOPS)], axis=1)

    def single(items):
        basis_one, blocks_one, window, leading_one = items
        projected = jnp.dot(basis_one, window, precision=lax.Precision.HIGHEST)
        summed = jnp.dot(projected, basis_one, precision=lax.Precision.HIGHEST)
        widened = blocks_one.astype(jnp.float32)
        summed = summed + jnp.einsum("hvw,hw->v", widened, leading_one, precision=lax.Precision.HIGHEST)
        backward = jnp.einsum("hvw,v->hw", widened, window, precision=lax.Precision.HIGHEST)
        return summed, backward

    totals, backs = lax.map(single, (sub_basis, blocks, windows, leading))
    backs = backs.reshape(N_ROW, N_COL, HOPS, W)
    for slot_index in range(HOPS):
        totals = totals + jnp.roll(backs[:, :, slot_index], slot_index + 1, axis=1).reshape(count, W)
    positions = offsets[:, None].astype(jnp.int32) + jnp.arange(W, dtype=jnp.int32)[None, :]
    result = jnp.zeros((N_COL, N_ROW * SLICE), jnp.float32)
    return result.at[columns[:, None], positions].add(totals)


def reference(sub_basis, coupling, pair_live, offsets, dual_in):
    blocks = form_blocks(sub_basis, coupling, pair_live)
    first_product = apply_dual(dual_in, sub_basis, blocks, offsets)
    return apply_dual(first_product, sub_basis, blocks, offsets)
```

```python
import jax
import jax.numpy as jnp
from jax import lax
from jax.experimental import pallas as pl
from jax.experimental.pallas import tpu as pltpu
from jax.sharding import PartitionSpec as P

LANES = 128
MESH = pl.DeviceIdType.MESH


def to_lanes(tile, chunks):
    wide = jnp.concatenate([jnp.broadcast_to(tile[j:j + 1, :], (8, LANES)) for j in range(chunks)], axis=1)
    high = wide.astype(jnp.bfloat16)
    row = lax.broadcasted_iota(jnp.int32, wide.shape, 0)
    return jnp.where(row % 2 == 0, high.astype(jnp.float32), wide - high.astype(jnp.float32)).astype(jnp.bfloat16)


def to_tile(vector, chunks):
    vector = vector + pltpu.roll(vector, 1, 0)
    row = lax.broadcasted_iota(jnp.int32, (8, LANES), 0)
    tile = jnp.zeros((8, LANES), jnp.float32)
    for j in range(chunks):
        tile = jnp.where(row == j, vector[:, j * LANES:(j + 1) * LANES], tile)
    return tile


def row_apply(rows, matrix):
    return jnp.dot(rows, matrix, preferred_element_type=jnp.float32)


def kernel(n_row, n_col, hops, basis_hbm, coupling_hbm, live_hbm, offset_hbm, dual_hbm, out_ref,
           mats, turned_basis, forward, backward, gathered, column, padded, all_offsets, packed,
           same_in, below_in, above_in, far_in, placing, outgoing, incoming, live_ref, offset_ref,
           load_sems, small_sems, dual_sems, offset_sems, pack_send, same_recv, below_recv, above_recv, far_recv,
           part_sems):
    me_row, me_col = lax.axis_index("row"), lax.axis_index("col")
    part_rows = dual_hbm.shape[0]
    rows = n_row * part_rows
    width = mats.shape[2]
    chunks = width // LANES
    kinds = hops + 1

    def peer(i, shift):
        return (lax.rem(me_row + i, n_row), lax.rem(me_col + (shift % n_col), n_col))

    def peers(shift):
        return [peer(i, shift) for i in range(n_row) if i > 0 or shift % n_col > 0]

    small = [
        pltpu.make_async_copy(dual_hbm, gathered.at[me_row], small_sems.at[0]),
        pltpu.make_async_copy(offset_hbm, offset_ref, small_sems.at[1]),
        pltpu.make_async_copy(live_hbm, live_ref, small_sems.at[2]),
    ]
    loads = [pltpu.make_async_copy(basis_hbm.at[0], mats.at[0], load_sems.at[0])]
    for h in range(hops):
        loads.append(pltpu.make_async_copy(coupling_hbm.at[0, h], mats.at[h + 1], load_sems.at[h + 1]))
    for copy in small:
        copy.start()

    barrier = pltpu.get_barrier_semaphore()
    greeted = 0
    for shift in sorted({d % n_col for d in range(-hops, hops + 1)}):
        for device in peers(shift):
            pl.semaphore_signal(barrier, inc=1, device_id=device, device_id_type=MESH)
            greeted += 1
    for load in loads:
        load.start()
    placing[...] = jnp.zeros(placing.shape, jnp.float32)
    padded[:, :, :8, :] = jnp.zeros((kinds, n_row, 8, LANES), jnp.float32)
    padded[:, :, 16:, :] = jnp.zeros((kinds, n_row, 8, LANES), jnp.float32)
    column[:, rows:, :] = jnp.zeros((kinds, column.shape[1] - rows, LANES), jnp.float32)
    for copy in small:
        copy.wait()
    all_offsets[me_row, 0] = offset_ref[0]

    def send(source, target, send_sem, recv_sem, device):
        pltpu.make_async_remote_copy(
            src_ref=source, dst_ref=target, send_sem=send_sem, recv_sem=recv_sem,
            device_id=device, device_id_type=MESH).start()

    def wait(ref, sem):
        pltpu.make_async_copy(ref, ref, sem).wait()

    def exchange_duals():
        pl.semaphore_wait(barrier, greeted)
        for k in range(kinds):
            for device in peers(-k):
                send(gathered.at[me_row], gathered.at[k * n_row + me_row], dual_sems.at[0], dual_sems.at[1], device)
        for k in list(range(1, kinds)):
            send(offset_ref, all_offsets.at[k * n_row + me_row], offset_sems.at[2], offset_sems.at[3], peer(0, -k))

    step = min(256, width)

    def form_matrices():
        for load in loads:
            load.wait()
        turned_basis[...] = mats[0].T
        for n in range(0, width, step):
            forward[0, :, n:n + step] = row_apply(turned_basis[...], mats[0, :, n:n + step]).astype(jnp.bfloat16)
        for h in range(hops):
            live = live_ref[0, h].astype(jnp.float32)
            for n in range(0, width, step):
                backward[h, :, n:n + step] = (
                    live * row_apply(turned_basis[...], mats[h + 1, :, n:n + step])).astype(jnp.bfloat16)
            forward[h + 1] = backward[h].T

    early = (lax.rem(me_row // 2, 2) + me_row // 4 + me_col >= 1).astype(jnp.int32)

    def opening(phase, carry):
        @pl.when(phase != early)
        def _():
            exchange_duals()

        @pl.when(phase == early)
        def _():
            form_matrices()
        return carry

    lax.fori_loop(0, 2, opening, 0)
    for k in range(kinds):
        for i in range(1, n_row):
            send(offset_ref, all_offsets.at[k * n_row + me_row], offset_sems.at[0], offset_sems.at[1], peer(i, -k))

    lane = lax.broadcasted_iota(jnp.int32, (8, LANES), 1)

    def cut_at(tile, within):
        turned = pltpu.roll(tile, lax.rem(LANES - within, LANES), 1)
        return jnp.where(lane < LANES - within, turned, pltpu.roll(turned, 7, 0))

    def moved_by(tile, within):
        turned = pltpu.roll(tile, within, 1)
        return jnp.where(lane >= within, turned, pltpu.roll(turned, 1, 0))

    spread_count = kinds * n_row - 1
    wait(gathered.at[pl.ds(0, spread_count)], dual_sems.at[1])
    wait(all_offsets.at[pl.ds(0, hops)], offset_sems.at[3])
    starts = [all_offsets[k * n_row + me_row, 0] for k in range(kinds)]
    firsts = [start // LANES for start in starts]
    withins = [start - first * LANES for start, first in zip(starts, firsts)]
    windows = []
    for k in range(kinds):
        for r in range(n_row):
            column[k, r * part_rows:(r + 1) * part_rows, :] = gathered[k * n_row + r]
        windows.append(cut_at(column[k, pl.ds(firsts[k], 8), :], withins[k]))

    def far_products(seen):
        return [moved_by(to_tile(row_apply(seen, backward[h]), chunks), withins[h + 1]) for h in range(hops)]

    def own_product(seen):
        vector = row_apply(seen[0], forward[0])
        for h in range(hops):
            vector = vector + row_apply(seen[h + 1], forward[h + 1])
        return moved_by(to_tile(vector, chunks), withins[0])

    seen = [to_lanes(window, chunks) for window in windows]
    back = far_products(seen[0])
    packed[32:48] = jnp.concatenate(back, axis=0).astype(jnp.bfloat16)
    for device in peers(1):
        send(packed.at[pl.ds(32, 16)], below_in.at[me_row], pack_send.at[0], below_recv.at[0], device)
    own = own_product(seen)
    packed[0:16] = jnp.concatenate([own, back[0]], axis=0).astype(jnp.bfloat16)
    packed[16:32] = jnp.concatenate([back[1], own], axis=0).astype(jnp.bfloat16)
    for shift in sorted({hops % n_col, -hops % n_col}):
        for device in peers(shift):
            slot = 0 if shift == hops % n_col else 1
            send(packed.at[pl.ds(16, 16)], far_in.at[slot, me_row], pack_send.at[1], far_recv.at[slot], device)
    for device in peers(-1):
        send(packed.at[pl.ds(0, 16)], above_in.at[me_row], pack_send.at[2], above_recv.at[0], device)
    for device in peers(0):
        send(packed.at[pl.ds(0, 32)], same_in.at[me_row], pack_send.at[3], same_recv.at[0], device)
    same_in[me_row] = packed[0:32]

    wait(all_offsets.at[pl.ds(0, kinds * (n_row - 1))], offset_sems.at[1])
    moves = [[jnp.clip(firsts[k] - all_offsets[k * n_row + r, 0] // LANES, -8, 8) for r in range(n_row)] for k in range(kinds)]
    far_slots = 1 if hops % n_col == -hops % n_col else 2
    wait(below_in, below_recv.at[0])
    for slot in range(far_slots):
        wait(far_in.at[slot], far_recv.at[slot])
    wait(above_in, above_recv.at[0])
    wait(same_in.at[pl.ds(0, n_row - 1)], same_recv.at[0])
    windows = []
    totals = [[], [], []]
    for r in range(n_row):
        same = same_in[r].astype(jnp.float32)
        below = below_in[r].astype(jnp.float32)
        above = above_in[r].astype(jnp.float32)
        low = far_in[0, r].astype(jnp.float32)
        high = low if far_slots == 1 else far_in[1, r].astype(jnp.float32)
        padded[0, r, 8:16, :] = same[0:8] + below[0:8] + low[0:8]
        padded[1, r, 8:16, :] = above[0:8] + same[8:16] + below[8:16]
        padded[2, r, 8:16, :] = high[8:16] + above[8:16] + same[16:24]
    for k in range(kinds):
        tile = padded[k, 0, pl.ds(8 + moves[k][0], 8), :]
        for r in range(1, n_row):
            tile = tile + padded[k, r, pl.ds(8 + moves[k][r], 8), :]
        windows.append(cut_at(tile, withins[k]))

    seen = [to_lanes(window, chunks) for window in windows]
    back = far_products(seen[0])

    def scatter(k, tile):
        placing[k, rows:rows + 8, :] = tile
        for i in range(n_row):
            device = peer(i, k)
            slot = device[0]
            piece = placing[k, pl.ds(rows - firsts[k] + slot * part_rows, part_rows), :]
            if k == 0 and i == 0:
                incoming[me_row] = piece
            else:
                outgoing[k * n_row + slot] = piece
                send(outgoing.at[k * n_row + slot], incoming.at[k * n_row + me_row], part_sems.at[0], part_sems.at[1], device)

    for h in reversed(range(hops)):
        scatter(h + 1, back[h])
    scatter(0, own_product(seen))
    wait(gathered.at[pl.ds(0, spread_count)], dual_sems.at[0])
    wait(all_offsets.at[pl.ds(0, kinds * (n_row - 1))], offset_sems.at[0])
    wait(all_offsets.at[pl.ds(0, hops)], offset_sems.at[2])
    wait(below_in, pack_send.at[0])
    for slot in range(far_slots):
        wait(far_in.at[slot], pack_send.at[1])
    wait(above_in, pack_send.at[2])
    wait(same_in.at[pl.ds(0, n_row - 1)], pack_send.at[3])
    wait(outgoing.at[pl.ds(0, spread_count)], part_sems.at[0])
    wait(incoming.at[pl.ds(0, spread_count)], part_sems.at[1])
    out_ref[...] = jnp.sum(incoming[...], axis=0)


def on_device(sub_basis, coupling, pair_live, offsets, dual_in):
    n_row, n_col = lax.axis_size("row"), lax.axis_size("col")
    hops = coupling.shape[1]
    kinds = hops + 1
    size = dual_in.shape[1]
    part_rows = size // LANES
    rows = n_row * part_rows
    depth, width = sub_basis.shape[1:]
    hbm = pl.BlockSpec(memory_space=pltpu.HBM)
    parts = pltpu.VMEM((kinds * n_row, part_rows, LANES), jnp.float32)
    pair = pltpu.VMEM((n_row, 16, LANES), jnp.bfloat16)
    dma = pltpu.SemaphoreType.DMA
    out = pl.pallas_call(
        lambda *refs: kernel(n_row, n_col, hops, *refs),
        out_shape=pltpu.VMEM((part_rows, LANES), jnp.float32),
        in_specs=[hbm] * 5,
        out_specs=pl.BlockSpec(memory_space=pltpu.VMEM),
        scratch_shapes=[
            pltpu.VMEM((kinds, depth, width), jnp.bfloat16),
            pltpu.VMEM((width, depth), jnp.bfloat16),
            pltpu.VMEM((kinds, width, width), jnp.bfloat16),
            pltpu.VMEM((hops, width, width), jnp.bfloat16),
            parts,
            pltpu.VMEM((kinds, rows + 8, LANES), jnp.float32),
            pltpu.VMEM((kinds, n_row, 24, LANES), jnp.float32),
            pltpu.SMEM((kinds * n_row, 1), jnp.int32),
            pltpu.VMEM((48, LANES), jnp.bfloat16),
            pltpu.VMEM((n_row, 32, LANES), jnp.bfloat16),
            pair, pair,
            pltpu.VMEM((2, n_row, 16, LANES), jnp.bfloat16),
            pltpu.VMEM((kinds, 2 * rows + 8, LANES), jnp.float32),
            parts, parts,
            pltpu.SMEM(pair_live.shape, jnp.int32),
            pltpu.SMEM(offsets.shape, jnp.int32),
            dma((kinds,)), dma((3,)), dma((2,)), dma((4,)), dma((4,)),
            dma((1,)), dma((1,)), dma((1,)), dma((2,)), dma((2,)),
        ],
        compiler_params=pltpu.CompilerParams(
            collective_id=0, has_side_effects=True, vmem_limit_bytes=60 * 1024 * 1024),
    )(sub_basis, coupling, pair_live, offsets, dual_in.reshape(part_rows, LANES))
    return out.reshape(1, size)


def solution(mesh):
    return jax.shard_map(
        on_device,
        mesh=mesh,
        in_specs=(
            P(("row", "col"), None, None),
            P(("row", "col"), None, None, None),
            P(("row", "col"), None),
            P(("row", "col")),
            P("col", "row"),
        ),
        out_specs=P("col", "row"),
        check_vma=False,
    )
```

```python
import jax
import jax.numpy as jnp
from jax import lax
from jax.experimental import pallas as pl
from jax.experimental.pallas import tpu as pltpu
from jax.sharding import PartitionSpec as P

LANES = 128
MESH = pl.DeviceIdType.MESH


def to_lanes(tile, chunks):
    wide = jnp.concatenate([jnp.broadcast_to(tile[j:j + 1, :], (8, LANES)) for j in range(chunks)], axis=1)
    high = wide.astype(jnp.bfloat16)
    row = lax.broadcasted_iota(jnp.int32, wide.shape, 0)
    return jnp.where(row % 2 == 0, high.astype(jnp.float32), wide - high.astype(jnp.float32)).astype(jnp.bfloat16)


def to_tile(vector, chunks):
    vector = vector + pltpu.roll(vector, 1, 0)
    row = lax.broadcasted_iota(jnp.int32, (8, LANES), 0)
    tile = jnp.zeros((8, LANES), jnp.float32)
    for j in range(chunks):
        tile = jnp.where(row == j, vector[:, j * LANES:(j + 1) * LANES], tile)
    return tile


def row_apply(rows, matrix):
    return jnp.dot(rows, matrix, preferred_element_type=jnp.float32)


def kernel(n_row, n_col, hops, basis_hbm, coupling_hbm, live_hbm, offset_hbm, dual_hbm, out_ref,
           mats, turned_basis, forward, backward, gathered, column, padded, all_offsets, packed,
           same_in, below_in, above_in, far_in, placing, outgoing, incoming, live_ref, offset_ref,
           load_sems, small_sems, dual_sems, offset_sems, pack_send, same_recv, below_recv, above_recv, far_recv,
           part_sems):
    me_row, me_col = lax.axis_index("row"), lax.axis_index("col")
    part_rows = dual_hbm.shape[0]
    rows = n_row * part_rows
    width = mats.shape[2]
    chunks = width // LANES
    kinds = hops + 1

    def peer(i, shift):
        return (lax.rem(me_row + i, n_row), lax.rem(me_col + (shift % n_col), n_col))

    def peers(shift):
        if shift % n_col == 0:
            return [peer(i, 0) for i in range(1, n_row)]
        return [(r, lax.rem(me_col + (shift % n_col), n_col)) for r in range(n_row)]

    small = [
        pltpu.make_async_copy(dual_hbm, gathered.at[me_row], small_sems.at[0]),
        pltpu.make_async_copy(offset_hbm, offset_ref, small_sems.at[1]),
        pltpu.make_async_copy(live_hbm, live_ref, small_sems.at[2]),
    ]
    loads = [pltpu.make_async_copy(basis_hbm.at[0], mats.at[0], load_sems.at[0])]
    for h in range(hops):
        loads.append(pltpu.make_async_copy(coupling_hbm.at[0, h], mats.at[h + 1], load_sems.at[h + 1]))
    for copy in small:
        copy.start()

    barrier = pltpu.get_barrier_semaphore()
    greeted = 0
    for shift in sorted({d % n_col for d in range(-hops, hops + 1)}):
        for device in peers(shift):
            pl.semaphore_signal(barrier, inc=1, device_id=device, device_id_type=MESH)
            greeted += 1
    for load in loads:
        load.start()
    placing[...] = jnp.zeros(placing.shape, jnp.float32)
    padded[:, :, :8, :] = jnp.zeros((kinds, n_row, 8, LANES), jnp.float32)
    padded[:, :, 16:, :] = jnp.zeros((kinds, n_row, 8, LANES), jnp.float32)
    column[:, rows:, :] = jnp.zeros((kinds, column.shape[1] - rows, LANES), jnp.float32)
    for copy in small:
        copy.wait()
    all_offsets[me_row, 0] = offset_ref[0]

    def send(source, target, send_sem, recv_sem, device):
        pltpu.make_async_remote_copy(
            src_ref=source, dst_ref=target, send_sem=send_sem, recv_sem=recv_sem,
            device_id=device, device_id_type=MESH).start()

    def wait(ref, sem):
        pltpu.make_async_copy(ref, ref, sem).wait()

    def exchange_duals():
        pl.semaphore_wait(barrier, greeted)
        for k in range(kinds):
            for device in peers(-k):
                send(gathered.at[me_row], gathered.at[k * n_row + me_row], dual_sems.at[0], dual_sems.at[1 + k], device)
        for k in list(range(1, kinds)):
            send(offset_ref, all_offsets.at[k * n_row + me_row], offset_sems.at[2], offset_sems.at[3], peer(0, -k))

    step = min(256, width)

    def form(m):
        pltpu.make_async_copy(mats.at[m], mats.at[m], load_sems.at[m]).wait()

        @pl.when(m == 0)
        def _():
            turned_basis[...] = mats[0].T
        scale = jnp.where(m == 0, 1, live_ref[0, jnp.maximum(m - 1, 0)]).astype(jnp.float32)
        for n in range(0, width, step):
            backward[m, :, n:n + step] = (
                scale * row_apply(turned_basis[...], mats[m, :, n:n + step])).astype(jnp.bfloat16)
        forward[m] = backward[m].T

    hop = lax.rem(me_row // 2, 2) + me_row // 4 + me_col
    turn = jnp.clip(3 - hop, 0, kinds)

    def opening(m, carry):
        @pl.when(m == turn)
        def _():
            exchange_duals()

        @pl.when(m < kinds)
        def _():
            form(m)
        return carry

    lax.fori_loop(0, kinds + 1, opening, 0)
    for k in range(kinds):
        for i in range(1, n_row):
            send(offset_ref, all_offsets.at[k * n_row + me_row], offset_sems.at[0], offset_sems.at[1], peer(i, -k))

    lane = lax.broadcasted_iota(jnp.int32, (8, LANES), 1)

    def cut_at(tile, within):
        turned = pltpu.roll(tile, lax.rem(LANES - within, LANES), 1)
        return jnp.where(lane < LANES - within, turned, pltpu.roll(turned, 7, 0))

    def moved_by(tile, within):
        turned = pltpu.roll(tile, within, 1)
        return jnp.where(lane >= within, turned, pltpu.roll(turned, 1, 0))

    spread_count = kinds * n_row - 1

    def window_of(k):
        wait(gathered.at[pl.ds(0, n_row if k > 0 else n_row - 1)], dual_sems.at[1 + k])
        if k == 1:
            wait(all_offsets.at[pl.ds(0, hops)], offset_sems.at[3])
        start = all_offsets[k * n_row + me_row, 0]
        for r in range(n_row):
            column[k, r * part_rows:(r + 1) * part_rows, :] = gathered[k * n_row + r]
        return cut_at(column[k, pl.ds(start // LANES, 8), :], lax.rem(start, LANES))

    def far_product(seen, h):
        return to_tile(row_apply(seen, backward[h + 1]), chunks)

    def own_product(seen):
        vector = row_apply(seen[0], forward[0])
        for h in range(hops):
            vector = vector + row_apply(seen[h + 1], forward[h + 1])
        return to_tile(vector, chunks)

    seen = [to_lanes(window_of(0), chunks)]
    back = [far_product(seen[0], h) for h in range(hops)]
    packed[32:48] = jnp.concatenate(back, axis=0).astype(jnp.bfloat16)
    for device in peers(1):
        send(packed.at[pl.ds(32, 16)], below_in.at[me_row], pack_send.at[0], below_recv.at[0], device)
    for k in range(1, kinds):
        seen.append(to_lanes(window_of(k), chunks))
    own = own_product(seen)
    packed[0:16] = jnp.concatenate([own, back[0]], axis=0).astype(jnp.bfloat16)
    packed[16:32] = jnp.concatenate([back[1], own], axis=0).astype(jnp.bfloat16)
    for shift in sorted({hops % n_col, -hops % n_col}):
        for device in peers(shift):
            slot = 0 if shift == hops % n_col else 1
            send(packed.at[pl.ds(16, 16)], far_in.at[slot, me_row], pack_send.at[1], far_recv.at[slot], device)
    for device in peers(-1):
        send(packed.at[pl.ds(0, 16)], above_in.at[me_row], pack_send.at[2], above_recv.at[0], device)
    for device in peers(0):
        send(packed.at[pl.ds(0, 32)], same_in.at[me_row], pack_send.at[3], same_recv.at[0], device)
    same_in[me_row] = packed[0:32]

    wait(all_offsets.at[pl.ds(0, kinds * (n_row - 1))], offset_sems.at[1])
    starts = [[all_offsets[k * n_row + r, 0] for r in range(n_row)] for k in range(kinds)]
    mine = [all_offsets[k * n_row + me_row, 0] for k in range(kinds)]
    firsts = [start // LANES for start in mine]
    withins = [lax.rem(start, LANES) for start in mine]
    moves = [[jnp.clip(firsts[k] - starts[k][r] // LANES, -8, 8) for r in range(n_row)] for k in range(kinds)]
    far_slots = 1 if hops % n_col == -hops % n_col else 2
    wait(below_in, below_recv.at[0])
    for slot in range(far_slots):
        wait(far_in.at[slot], far_recv.at[slot])
    wait(above_in, above_recv.at[0])
    wait(same_in.at[pl.ds(0, n_row - 1)], same_recv.at[0])
    windows = []
    for r in range(n_row):
        same = same_in[r].astype(jnp.float32)
        below = below_in[r].astype(jnp.float32)
        above = above_in[r].astype(jnp.float32)
        low = far_in[0, r].astype(jnp.float32)
        high = low if far_slots == 1 else far_in[1, r].astype(jnp.float32)
        padded[0, r, 8:16, :] = moved_by(same[0:8] + below[0:8] + low[0:8], lax.rem(starts[0][r], LANES))
        padded[1, r, 8:16, :] = moved_by(above[0:8] + same[8:16] + below[8:16], lax.rem(starts[1][r], LANES))
        padded[2, r, 8:16, :] = moved_by(high[8:16] + above[8:16] + same[16:24], lax.rem(starts[2][r], LANES))
    for k in range(kinds):
        tile = padded[k, 0, pl.ds(8 + moves[k][0], 8), :]
        for r in range(1, n_row):
            tile = tile + padded[k, r, pl.ds(8 + moves[k][r], 8), :]
        windows.append(cut_at(tile, withins[k]))

    seen = [to_lanes(window, chunks) for window in windows]
    back = [far_product(seen[0], h) for h in range(hops)]

    def scatter(k, tile):
        placing[k, rows:rows + 8, :] = moved_by(tile, withins[k])
        for i in range(n_row):
            device = peer(i, k) if k == 0 else (i, peer(0, k)[1])
            slot = device[0]
            piece = placing[k, pl.ds(rows - firsts[k] + slot * part_rows, part_rows), :]
            if k == 0 and i == 0:
                incoming[me_row] = piece
            else:
                outgoing[k * n_row + slot] = piece
                send(outgoing.at[k * n_row + slot], incoming.at[k * n_row + me_row], part_sems.at[0], part_sems.at[1], device)

    for h in reversed(range(hops)):
        scatter(h + 1, back[h])
    scatter(0, own_product(seen))
    wait(gathered.at[pl.ds(0, spread_count)], dual_sems.at[0])
    wait(all_offsets.at[pl.ds(0, kinds * (n_row - 1))], offset_sems.at[0])
    wait(all_offsets.at[pl.ds(0, hops)], offset_sems.at[2])
    wait(below_in, pack_send.at[0])
    for slot in range(far_slots):
        wait(far_in.at[slot], pack_send.at[1])
    wait(above_in, pack_send.at[2])
    wait(same_in.at[pl.ds(0, n_row - 1)], pack_send.at[3])
    wait(outgoing.at[pl.ds(0, spread_count)], part_sems.at[0])
    wait(incoming.at[pl.ds(0, spread_count)], part_sems.at[1])
    out_ref[...] = jnp.sum(incoming[...], axis=0)


def on_device(sub_basis, coupling, pair_live, offsets, dual_in):
    n_row, n_col = lax.axis_size("row"), lax.axis_size("col")
    hops = coupling.shape[1]
    kinds = hops + 1
    size = dual_in.shape[1]
    part_rows = size // LANES
    rows = n_row * part_rows
    depth, width = sub_basis.shape[1:]
    hbm = pl.BlockSpec(memory_space=pltpu.HBM)
    parts = pltpu.VMEM((kinds * n_row, part_rows, LANES), jnp.float32)
    pair = pltpu.VMEM((n_row, 16, LANES), jnp.bfloat16)
    dma = pltpu.SemaphoreType.DMA
    out = pl.pallas_call(
        lambda *refs: kernel(n_row, n_col, hops, *refs),
        out_shape=pltpu.VMEM((part_rows, LANES), jnp.float32),
        in_specs=[hbm] * 5,
        out_specs=pl.BlockSpec(memory_space=pltpu.VMEM),
        scratch_shapes=[
            pltpu.VMEM((kinds, depth, width), jnp.bfloat16),
            pltpu.VMEM((width, depth), jnp.bfloat16),
            pltpu.VMEM((kinds, width, width), jnp.bfloat16),
            pltpu.VMEM((kinds, width, width), jnp.bfloat16),
            parts,
            pltpu.VMEM((kinds, rows + 8, LANES), jnp.float32),
            pltpu.VMEM((kinds, n_row, 24, LANES), jnp.float32),
            pltpu.SMEM((kinds * n_row, 1), jnp.int32),
            pltpu.VMEM((48, LANES), jnp.bfloat16),
            pltpu.VMEM((n_row, 32, LANES), jnp.bfloat16),
            pair, pair,
            pltpu.VMEM((2, n_row, 16, LANES), jnp.bfloat16),
            pltpu.VMEM((kinds, 2 * rows + 8, LANES), jnp.float32),
            parts, parts,
            pltpu.SMEM(pair_live.shape, jnp.int32),
            pltpu.SMEM(offsets.shape, jnp.int32),
            dma((kinds,)), dma((3,)), dma((kinds + 1,)), dma((4,)), dma((4,)),
            dma((1,)), dma((1,)), dma((1,)), dma((2,)), dma((2,)),
        ],
        compiler_params=pltpu.CompilerParams(
            collective_id=0, has_side_effects=True, vmem_limit_bytes=60 * 1024 * 1024),
    )(sub_basis, coupling, pair_live, offsets, dual_in.reshape(part_rows, LANES))
    return out.reshape(1, size)


def solution(mesh):
    return jax.shard_map(
        on_device,
        mesh=mesh,
        in_specs=(
            P(("row", "col"), None, None),
            P(("row", "col"), None, None, None),
            P(("row", "col"), None),
            P(("row", "col")),
            P("col", "row"),
        ),
        out_specs=P("col", "row"),
        check_vma=False,
    )
```

```python
import jax
import jax.numpy as jnp
from jax import lax
from jax.experimental import pallas as pl
from jax.experimental.pallas import tpu as pltpu
from jax.sharding import PartitionSpec as P

LANES = 128
MESH = pl.DeviceIdType.MESH


def to_lanes(tile, chunks):
    wide = jnp.concatenate([jnp.broadcast_to(tile[j:j + 1, :], (8, LANES)) for j in range(chunks)], axis=1)
    high = wide.astype(jnp.bfloat16)
    row = lax.broadcasted_iota(jnp.int32, wide.shape, 0)
    return jnp.where(row % 2 == 0, high.astype(jnp.float32), wide - high.astype(jnp.float32)).astype(jnp.bfloat16)


def to_tile(vector, chunks):
    vector = vector + pltpu.roll(vector, 1, 0)
    row = lax.broadcasted_iota(jnp.int32, (8, LANES), 0)
    tile = jnp.zeros((8, LANES), jnp.float32)
    for j in range(chunks):
        tile = jnp.where(row == j, vector[:, j * LANES:(j + 1) * LANES], tile)
    return tile


def row_apply(rows, matrix):
    return jnp.dot(rows, matrix, preferred_element_type=jnp.float32)


def kernel(n_row, n_col, hops, basis_hbm, coupling_hbm, live_hbm, offset_hbm, dual_hbm, out_ref,
           mats, turned_basis, forward, backward, gathered, column, padded, all_offsets, packed,
           plain, pair_in, below_in, above_in, own_in, far_own_in, far_back_in, placing, outgoing, incoming,
           live_ref, offset_ref, load_sems, small_sems, dual_sems, offset_sems, pack_send, pack_recv, part_sems):
    me_row, me_col = lax.axis_index("row"), lax.axis_index("col")
    part_rows = dual_hbm.shape[0]
    rows = n_row * part_rows
    width = mats.shape[2]
    chunks = width // LANES
    kinds = hops + 1

    def peer(i, shift):
        return (lax.rem(me_row + i, n_row), lax.rem(me_col + (shift % n_col), n_col))

    def peers(shift):
        if shift % n_col == 0:
            return [peer(i, 0) for i in range(1, n_row)]
        return [(r, lax.rem(me_col + (shift % n_col), n_col)) for r in range(n_row)]

    small = [
        pltpu.make_async_copy(dual_hbm, gathered.at[me_row], small_sems.at[0]),
        pltpu.make_async_copy(offset_hbm, offset_ref, small_sems.at[1]),
        pltpu.make_async_copy(live_hbm, live_ref, small_sems.at[2]),
    ]
    loads = [pltpu.make_async_copy(basis_hbm.at[0], mats.at[0], load_sems.at[0])]
    for h in range(hops):
        loads.append(pltpu.make_async_copy(coupling_hbm.at[0, h], mats.at[h + 1], load_sems.at[h + 1]))
    for copy in small:
        copy.start()

    barrier = pltpu.get_barrier_semaphore()
    greeted = 0
    for shift in sorted({d % n_col for d in range(-hops, hops + 1)}):
        for device in peers(shift):
            pl.semaphore_signal(barrier, inc=1, device_id=device, device_id_type=MESH)
            greeted += 1
    for load in loads:
        load.start()
    placing[...] = jnp.zeros(placing.shape, jnp.float32)
    padded[:, :, :8, :] = jnp.zeros((kinds, n_row, 8, LANES), jnp.float32)
    padded[:, :, 16:, :] = jnp.zeros((kinds, n_row, 8, LANES), jnp.float32)
    column[:, rows:, :] = jnp.zeros((kinds, column.shape[1] - rows, LANES), jnp.float32)
    for ref in (own_in, far_own_in, far_back_in):
        ref[:, chunks:, :] = jnp.zeros((n_row, 8 - chunks, LANES), jnp.float32)
    for copy in small:
        copy.wait()
    all_offsets[me_row, 0] = offset_ref[0]

    def send(source, target, send_sem, recv_sem, device):
        pltpu.make_async_remote_copy(
            src_ref=source, dst_ref=target, send_sem=send_sem, recv_sem=recv_sem,
            device_id=device, device_id_type=MESH).start()

    def wait(ref, sem):
        pltpu.make_async_copy(ref, ref, sem).wait()

    def exchange_duals():
        pl.semaphore_wait(barrier, greeted)
        for k in range(kinds):
            for device in peers(-k):
                send(gathered.at[me_row], gathered.at[k * n_row + me_row], dual_sems.at[0], dual_sems.at[1 + k], device)
        for k in list(range(1, kinds)):
            send(offset_ref, all_offsets.at[k * n_row + me_row], offset_sems.at[2], offset_sems.at[3], peer(0, -k))

    step = min(256, width)

    def form(m):
        pltpu.make_async_copy(mats.at[m], mats.at[m], load_sems.at[m]).wait()

        @pl.when(m == 0)
        def _():
            turned_basis[...] = mats[0].T
        scale = jnp.where(m == 0, 1, live_ref[0, jnp.maximum(m - 1, 0)]).astype(jnp.float32)
        for n in range(0, width, step):
            backward[m, :, n:n + step] = (
                scale * row_apply(turned_basis[...], mats[m, :, n:n + step])).astype(jnp.bfloat16)
        forward[m] = backward[m].T

    hop = lax.rem(me_row // 2, 2) + me_row // 4 + me_col
    turn = jnp.clip(3 - hop, 0, kinds)

    def opening(m, carry):
        @pl.when(m == turn)
        def _():
            exchange_duals()

        @pl.when(m < kinds)
        def _():
            form(m)
        return carry

    lax.fori_loop(0, kinds + 1, opening, 0)
    for k in range(kinds):
        for i in range(1, n_row):
            send(offset_ref, all_offsets.at[k * n_row + me_row], offset_sems.at[0], offset_sems.at[1], peer(i, -k))

    lane = lax.broadcasted_iota(jnp.int32, (8, LANES), 1)

    def cut_at(tile, within):
        turned = pltpu.roll(tile, lax.rem(LANES - within, LANES), 1)
        return jnp.where(lane < LANES - within, turned, pltpu.roll(turned, 7, 0))

    def moved_by(tile, within):
        turned = pltpu.roll(tile, within, 1)
        return jnp.where(lane >= within, turned, pltpu.roll(turned, 1, 0))

    spread_count = kinds * n_row - 1

    def window_of(k):
        wait(gathered.at[pl.ds(0, n_row if k > 0 else n_row - 1)], dual_sems.at[1 + k])
        if k == 1:
            wait(all_offsets.at[pl.ds(0, hops)], offset_sems.at[3])
        start = all_offsets[k * n_row + me_row, 0]
        for r in range(n_row):
            column[k, r * part_rows:(r + 1) * part_rows, :] = gathered[k * n_row + r]
        return cut_at(column[k, pl.ds(start // LANES, 8), :], lax.rem(start, LANES))

    def far_product(seen, h):
        return to_tile(row_apply(seen, backward[h + 1]), chunks)

    def own_product(seen):
        vector = row_apply(seen[0], forward[0])
        for h in range(hops):
            vector = vector + row_apply(seen[h + 1], forward[h + 1])
        return to_tile(vector, chunks)

    def pass_on(source, target, which, devices):
        for device in devices:
            send(source, target, pack_send.at[which], pack_recv.at[which], device)

    used = pl.ds(0, chunks)
    seen = [to_lanes(window_of(0), chunks)]
    back = [far_product(seen[0], h) for h in range(hops)]
    pair = jnp.concatenate(back, axis=0).astype(jnp.bfloat16)
    packed[0:16] = pair
    pair_in[me_row] = pair
    pass_on(packed.at[pl.ds(0, 16)], below_in.at[me_row], 1, peers(1))
    plain[0] = back[1]
    pass_on(plain.at[0, used], far_back_in.at[me_row, used], 0, peers(2))
    inner = row_apply(seen[0], forward[0])
    for k in range(1, kinds):
        inner = inner + row_apply(to_lanes(window_of(k), chunks), forward[k])
    own = to_tile(inner, chunks)
    plain[1] = own
    own_in[me_row] = own
    pass_on(plain.at[1, used], own_in.at[me_row, used], 2, peers(0))
    pass_on(packed.at[pl.ds(0, 16)], pair_in.at[me_row], 3, peers(0))
    packed[16:32] = jnp.concatenate([own, back[0]], axis=0).astype(jnp.bfloat16)
    pass_on(packed.at[pl.ds(16, 16)], above_in.at[me_row], 4, peers(-1))
    pass_on(plain.at[1, used], far_own_in.at[me_row, used], 5, peers(-2))

    wait(all_offsets.at[pl.ds(0, kinds * (n_row - 1))], offset_sems.at[1])
    starts = [[all_offsets[k * n_row + r, 0] for r in range(n_row)] for k in range(kinds)]
    mine = [all_offsets[k * n_row + me_row, 0] for k in range(kinds)]
    firsts = [start // LANES for start in mine]
    withins = [lax.rem(start, LANES) for start in mine]
    moves = [[jnp.clip(firsts[k] - starts[k][r] // LANES, -8, 8) for r in range(n_row)] for k in range(kinds)]
    def gather_window(k, parts_of):
        for r in range(n_row):
            padded[k, r, 8:16, :] = moved_by(parts_of(r), lax.rem(starts[k][r], LANES))
        tile = padded[k, 0, pl.ds(8 + moves[k][0], 8), :]
        for r in range(1, n_row):
            tile = tile + padded[k, r, pl.ds(8 + moves[k][r], 8), :]
        return to_lanes(cut_at(tile, withins[k]), chunks)

    def wide(ref):
        return ref.astype(jnp.float32)

    wait(below_in, pack_recv.at[1])
    wait(own_in.at[pl.ds(0, n_row - 1), used], pack_recv.at[2])
    wait(far_back_in.at[:, used], pack_recv.at[0])
    seen = [gather_window(0, lambda r: own_in[r] + wide(below_in[r])[0:8] + far_back_in[r])]
    back = [far_product(seen[0], h) for h in range(hops)]

    def scatter(k, tile):
        placing[k, rows:rows + 8, :] = moved_by(tile, withins[k])
        for i in range(n_row):
            device = peer(i, k) if k == 0 else (i, peer(0, k)[1])
            slot = device[0]
            piece = placing[k, pl.ds(rows - firsts[k] + slot * part_rows, part_rows), :]
            if k == 0 and i == 0:
                incoming[me_row] = piece
            else:
                outgoing[k * n_row + slot] = piece
                send(outgoing.at[k * n_row + slot], incoming.at[k * n_row + me_row], part_sems.at[0], part_sems.at[1], device)

    for h in range(hops):
        scatter(h + 1, back[h])
    wait(pair_in.at[pl.ds(0, n_row - 1)], pack_recv.at[3])
    wait(above_in, pack_recv.at[4])
    wait(far_own_in.at[:, used], pack_recv.at[5])
    seen.append(gather_window(1, lambda r: (
        wide(above_in[r])[0:8] + wide(pair_in[r])[0:8] + wide(below_in[r])[8:16])))
    seen.append(gather_window(2, lambda r: (
        far_own_in[r] + wide(above_in[r])[8:16] + wide(pair_in[r])[8:16])))
    scatter(0, own_product(seen))
    wait(gathered.at[pl.ds(0, spread_count)], dual_sems.at[0])
    wait(all_offsets.at[pl.ds(0, kinds * (n_row - 1))], offset_sems.at[0])
    wait(all_offsets.at[pl.ds(0, hops)], offset_sems.at[2])
    wait(far_back_in.at[:, used], pack_send.at[0])
    wait(below_in, pack_send.at[1])
    wait(own_in.at[pl.ds(0, n_row - 1), used], pack_send.at[2])
    wait(pair_in.at[pl.ds(0, n_row - 1)], pack_send.at[3])
    wait(above_in, pack_send.at[4])
    wait(far_own_in.at[:, used], pack_send.at[5])
    wait(outgoing.at[pl.ds(0, spread_count)], part_sems.at[0])
    wait(incoming.at[pl.ds(0, spread_count)], part_sems.at[1])
    out_ref[...] = jnp.sum(incoming[...], axis=0)


def on_device(sub_basis, coupling, pair_live, offsets, dual_in):
    n_row, n_col = lax.axis_size("row"), lax.axis_size("col")
    hops = coupling.shape[1]
    kinds = hops + 1
    size = dual_in.shape[1]
    part_rows = size // LANES
    rows = n_row * part_rows
    depth, width = sub_basis.shape[1:]
    hbm = pl.BlockSpec(memory_space=pltpu.HBM)
    parts = pltpu.VMEM((kinds * n_row, part_rows, LANES), jnp.float32)
    pair = pltpu.VMEM((n_row, 16, LANES), jnp.bfloat16)
    single = pltpu.VMEM((n_row, 8, LANES), jnp.float32)
    dma = pltpu.SemaphoreType.DMA
    out = pl.pallas_call(
        lambda *refs: kernel(n_row, n_col, hops, *refs),
        out_shape=pltpu.VMEM((part_rows, LANES), jnp.float32),
        in_specs=[hbm] * 5,
        out_specs=pl.BlockSpec(memory_space=pltpu.VMEM),
        scratch_shapes=[
            pltpu.VMEM((kinds, depth, width), jnp.bfloat16),
            pltpu.VMEM((width, depth), jnp.bfloat16),
            pltpu.VMEM((kinds, width, width), jnp.bfloat16),
            pltpu.VMEM((kinds, width, width), jnp.bfloat16),
            parts,
            pltpu.VMEM((kinds, rows + 8, LANES), jnp.float32),
            pltpu.VMEM((kinds, n_row, 24, LANES), jnp.float32),
            pltpu.SMEM((kinds * n_row, 1), jnp.int32),
            pltpu.VMEM((32, LANES), jnp.bfloat16),
            pltpu.VMEM((2, 8, LANES), jnp.float32),
            pair, pair, pair,
            single, single, single,
            pltpu.VMEM((kinds, 2 * rows + 8, LANES), jnp.float32),
            parts, parts,
            pltpu.SMEM(pair_live.shape, jnp.int32),
            pltpu.SMEM(offsets.shape, jnp.int32),
            dma((kinds,)), dma((3,)), dma((kinds + 1,)), dma((4,)), dma((6,)), dma((6,)), dma((2,)),
        ],
        compiler_params=pltpu.CompilerParams(
            collective_id=0, has_side_effects=True, vmem_limit_bytes=60 * 1024 * 1024),
    )(sub_basis, coupling, pair_live, offsets, dual_in.reshape(part_rows, LANES))
    return out.reshape(1, size)


def solution(mesh):
    return jax.shard_map(
        on_device,
        mesh=mesh,
        in_specs=(
            P(("row", "col"), None, None),
            P(("row", "col"), None, None, None),
            P(("row", "col"), None),
            P(("row", "col")),
            P("col", "row"),
        ),
        out_specs=P("col", "row"),
        check_vma=False,
    )
```

```python
import jax
import jax.numpy as jnp
from jax import lax
from jax.experimental import pallas as pl
from jax.experimental.pallas import tpu as pltpu
from jax.sharding import PartitionSpec as P

LANES = 128
MESH = pl.DeviceIdType.MESH


def to_lanes(tile, chunks):
    wide = jnp.concatenate([jnp.broadcast_to(tile[j:j + 1, :], (8, LANES)) for j in range(chunks)], axis=1)
    high = wide.astype(jnp.bfloat16)
    row = lax.broadcasted_iota(jnp.int32, wide.shape, 0)
    return jnp.where(row % 2 == 0, high.astype(jnp.float32), wide - high.astype(jnp.float32)).astype(jnp.bfloat16)


def halves(wide):
    high = wide.astype(jnp.bfloat16).astype(jnp.float32)
    row = lax.broadcasted_iota(jnp.int32, wide.shape, 0)
    return jnp.where(row % 2 == 0, high, wide - high).astype(jnp.bfloat16)


def to_tile(vector, chunks):
    vector = vector + pltpu.roll(vector, 1, 0)
    row = lax.broadcasted_iota(jnp.int32, (8, LANES), 0)
    tile = jnp.zeros((8, LANES), jnp.float32)
    for j in range(chunks):
        tile = jnp.where(row == j, vector[:, j * LANES:(j + 1) * LANES], tile)
    return tile


def row_apply(rows, matrix):
    return jnp.dot(rows, matrix, preferred_element_type=jnp.float32)


def kernel(n_row, n_col, hops, basis_hbm, coupling_hbm, live_hbm, offset_hbm, dual_hbm, out_ref,
           mats, turned_basis, forward, backward, gathered, column, padded, all_offsets, packed,
           plain, pair_in, below_in, above_in, own_in, far_own_in, far_back_in, placing, outgoing, incoming,
           live_ref, offset_ref, load_sems, small_sems, dual_sems, offset_sems, pack_send, pack_recv, part_sems):
    me_row, me_col = lax.axis_index("row"), lax.axis_index("col")
    part_rows = dual_hbm.shape[0]
    rows = n_row * part_rows
    width = mats.shape[2]
    chunks = width // LANES
    kinds = hops + 1

    def peer(i, shift):
        return (lax.rem(me_row + i, n_row), lax.rem(me_col + (shift % n_col), n_col))

    def peers(shift):
        if shift % n_col == 0:
            return [peer(i, 0) for i in range(1, n_row)]
        return [(r, lax.rem(me_col + (shift % n_col), n_col)) for r in range(n_row)]

    small = [
        pltpu.make_async_copy(dual_hbm, gathered.at[me_row], small_sems.at[0]),
        pltpu.make_async_copy(offset_hbm, offset_ref, small_sems.at[1]),
        pltpu.make_async_copy(live_hbm, live_ref, small_sems.at[2]),
    ]
    loads = [pltpu.make_async_copy(basis_hbm.at[0], mats.at[0], load_sems.at[0])]
    for h in range(hops):
        loads.append(pltpu.make_async_copy(coupling_hbm.at[0, h], mats.at[h + 1], load_sems.at[h + 1]))
    for copy in small:
        copy.start()

    barrier = pltpu.get_barrier_semaphore()
    greeted = 0
    for shift in sorted({d % n_col for d in range(-hops, hops + 1)}):
        for device in peers(shift):
            pl.semaphore_signal(barrier, inc=1, device_id=device, device_id_type=MESH)
            greeted += 1
    for load in loads:
        load.start()
    placing[...] = jnp.zeros(placing.shape, jnp.float32)
    padded[:, :, :8, :] = jnp.zeros((kinds, n_row, 8, LANES), jnp.float32)
    padded[:, :, 16:, :] = jnp.zeros((kinds, n_row, 8, LANES), jnp.float32)
    column[:, rows:, :] = jnp.zeros((kinds, column.shape[1] - rows, LANES), jnp.float32)
    for ref in (own_in, far_own_in, far_back_in):
        ref[:, chunks:, :] = jnp.zeros((n_row, 8 - chunks, LANES), jnp.float32)
    for copy in small:
        copy.wait()
    all_offsets[me_row, 0] = offset_ref[0]

    def send(source, target, send_sem, recv_sem, device):
        pltpu.make_async_remote_copy(
            src_ref=source, dst_ref=target, send_sem=send_sem, recv_sem=recv_sem,
            device_id=device, device_id_type=MESH).start()

    def wait(ref, sem):
        pltpu.make_async_copy(ref, ref, sem).wait()

    def exchange_duals():
        pl.semaphore_wait(barrier, greeted)
        for k in range(kinds):
            for device in peers(-k):
                send(gathered.at[me_row], gathered.at[k * n_row + me_row], dual_sems.at[0], dual_sems.at[1 + k], device)
        for k in list(range(1, kinds)):
            send(offset_ref, all_offsets.at[k * n_row + me_row], offset_sems.at[2], offset_sems.at[3], peer(0, -k))

    step = min(256, width)

    def form(m):
        pltpu.make_async_copy(mats.at[m], mats.at[m], load_sems.at[m]).wait()

        @pl.when(m == 0)
        def _():
            turned_basis[...] = mats[0].T
        @pl.when(m > 0)
        def _():
            live = live_ref[0, jnp.maximum(m - 1, 0)].astype(jnp.float32)
            for n in range(0, width, step):
                backward[m, :, n:n + step] = (
                    live * row_apply(turned_basis[...], mats[m, :, n:n + step])).astype(jnp.bfloat16)
            forward[m] = backward[m].T

    hop = lax.rem(me_row // 2, 2) + me_row // 4 + me_col
    turn = jnp.clip(3 - hop, 0, kinds)

    def opening(m, carry):
        @pl.when(m == turn)
        def _():
            exchange_duals()

        @pl.when(m < kinds)
        def _():
            form(m)
        return carry

    lax.fori_loop(0, kinds + 1, opening, 0)
    for k in range(kinds):
        for i in range(1, n_row):
            send(offset_ref, all_offsets.at[k * n_row + me_row], offset_sems.at[0], offset_sems.at[1], peer(i, -k))

    lane = lax.broadcasted_iota(jnp.int32, (8, LANES), 1)

    def cut_at(tile, within):
        turned = pltpu.roll(tile, lax.rem(LANES - within, LANES), 1)
        return jnp.where(lane < LANES - within, turned, pltpu.roll(turned, 7, 0))

    def moved_by(tile, within):
        turned = pltpu.roll(tile, within, 1)
        return jnp.where(lane >= within, turned, pltpu.roll(turned, 1, 0))

    spread_count = kinds * n_row - 1

    def window_of(k):
        wait(gathered.at[pl.ds(0, n_row if k > 0 else n_row - 1)], dual_sems.at[1 + k])
        if k == 1:
            wait(all_offsets.at[pl.ds(0, hops)], offset_sems.at[3])
        start = all_offsets[k * n_row + me_row, 0]
        for r in range(n_row):
            column[k, r * part_rows:(r + 1) * part_rows, :] = gathered[k * n_row + r]
        return cut_at(column[k, pl.ds(start // LANES, 8), :], lax.rem(start, LANES))

    def far_product(seen, h):
        return to_tile(row_apply(seen, backward[h + 1]), chunks)

    def basis_product(row):
        vector = row_apply(row, turned_basis[...])
        return row_apply(halves(vector + pltpu.roll(vector, 1, 0)), mats[0])

    def own_product(seen):
        vector = basis_product(seen[0])
        for h in range(hops):
            vector = vector + row_apply(seen[h + 1], forward[h + 1])
        return to_tile(vector, chunks)

    def pass_on(source, target, which, devices):
        for device in devices:
            send(source, target, pack_send.at[which], pack_recv.at[which], device)

    used = pl.ds(0, chunks)
    seen = [to_lanes(window_of(0), chunks)]
    back = [far_product(seen[0], h) for h in range(hops)]
    pair = jnp.concatenate(back, axis=0).astype(jnp.bfloat16)
    packed[0:16] = pair
    pair_in[me_row] = pair
    pass_on(packed.at[pl.ds(0, 16)], below_in.at[me_row], 1, peers(1))
    plain[0] = back[1]
    pass_on(plain.at[0, used], far_back_in.at[me_row, used], 0, peers(2))
    inner = basis_product(seen[0])
    for k in range(1, kinds):
        inner = inner + row_apply(to_lanes(window_of(k), chunks), forward[k])
    own = to_tile(inner, chunks)
    plain[1] = own
    own_in[me_row] = own
    pass_on(plain.at[1, used], own_in.at[me_row, used], 2, peers(0))
    pass_on(packed.at[pl.ds(0, 16)], pair_in.at[me_row], 3, peers(0))
    packed[16:32] = jnp.concatenate([own, back[0]], axis=0).astype(jnp.bfloat16)
    pass_on(packed.at[pl.ds(16, 16)], above_in.at[me_row], 4, peers(-1))
    pass_on(plain.at[1, used], far_own_in.at[me_row, used], 5, peers(-2))

    wait(all_offsets.at[pl.ds(0, kinds * (n_row - 1))], offset_sems.at[1])
    starts = [[all_offsets[k * n_row + r, 0] for r in range(n_row)] for k in range(kinds)]
    mine = [all_offsets[k * n_row + me_row, 0] for k in range(kinds)]
    firsts = [start // LANES for start in mine]
    withins = [lax.rem(start, LANES) for start in mine]
    moves = [[jnp.clip(firsts[k] - starts[k][r] // LANES, -8, 8) for r in range(n_row)] for k in range(kinds)]
    def gather_window(k, parts_of):
        for r in range(n_row):
            padded[k, r, 8:16, :] = moved_by(parts_of(r), lax.rem(starts[k][r], LANES))
        tile = padded[k, 0, pl.ds(8 + moves[k][0], 8), :]
        for r in range(1, n_row):
            tile = tile + padded[k, r, pl.ds(8 + moves[k][r], 8), :]
        return to_lanes(cut_at(tile, withins[k]), chunks)

    def wide(ref):
        return ref.astype(jnp.float32)

    wait(below_in, pack_recv.at[1])
    wait(own_in.at[pl.ds(0, n_row - 1), used], pack_recv.at[2])
    wait(far_back_in.at[:, used], pack_recv.at[0])
    seen = [gather_window(0, lambda r: own_in[r] + wide(below_in[r])[0:8] + far_back_in[r])]
    back = [far_product(seen[0], h) for h in range(hops)]

    def scatter(k, tile):
        placing[k, rows:rows + 8, :] = moved_by(tile, withins[k])
        for i in range(n_row):
            device = peer(i, k) if k == 0 else (i, peer(0, k)[1])
            slot = device[0]
            piece = placing[k, pl.ds(rows - firsts[k] + slot * part_rows, part_rows), :]
            if k == 0 and i == 0:
                incoming[me_row] = piece
            else:
                outgoing[k * n_row + slot] = piece
                send(outgoing.at[k * n_row + slot], incoming.at[k * n_row + me_row], part_sems.at[0], part_sems.at[1], device)

    for h in range(hops):
        scatter(h + 1, back[h])
    wait(pair_in.at[pl.ds(0, n_row - 1)], pack_recv.at[3])
    wait(above_in, pack_recv.at[4])
    wait(far_own_in.at[:, used], pack_recv.at[5])
    seen.append(gather_window(1, lambda r: (
        wide(above_in[r])[0:8] + wide(pair_in[r])[0:8] + wide(below_in[r])[8:16])))
    seen.append(gather_window(2, lambda r: (
        far_own_in[r] + wide(above_in[r])[8:16] + wide(pair_in[r])[8:16])))
    scatter(0, own_product(seen))
    wait(gathered.at[pl.ds(0, spread_count)], dual_sems.at[0])
    wait(all_offsets.at[pl.ds(0, kinds * (n_row - 1))], offset_sems.at[0])
    wait(all_offsets.at[pl.ds(0, hops)], offset_sems.at[2])
    wait(far_back_in.at[:, used], pack_send.at[0])
    wait(below_in, pack_send.at[1])
    wait(own_in.at[pl.ds(0, n_row - 1), used], pack_send.at[2])
    wait(pair_in.at[pl.ds(0, n_row - 1)], pack_send.at[3])
    wait(above_in, pack_send.at[4])
    wait(far_own_in.at[:, used], pack_send.at[5])
    wait(outgoing.at[pl.ds(0, spread_count)], part_sems.at[0])
    wait(incoming.at[pl.ds(0, spread_count)], part_sems.at[1])
    out_ref[...] = jnp.sum(incoming[...], axis=0)


def on_device(sub_basis, coupling, pair_live, offsets, dual_in):
    n_row, n_col = lax.axis_size("row"), lax.axis_size("col")
    hops = coupling.shape[1]
    kinds = hops + 1
    size = dual_in.shape[1]
    part_rows = size // LANES
    rows = n_row * part_rows
    depth, width = sub_basis.shape[1:]
    hbm = pl.BlockSpec(memory_space=pltpu.HBM)
    parts = pltpu.VMEM((kinds * n_row, part_rows, LANES), jnp.float32)
    pair = pltpu.VMEM((n_row, 16, LANES), jnp.bfloat16)
    single = pltpu.VMEM((n_row, 8, LANES), jnp.float32)
    dma = pltpu.SemaphoreType.DMA
    out = pl.pallas_call(
        lambda *refs: kernel(n_row, n_col, hops, *refs),
        out_shape=pltpu.VMEM((part_rows, LANES), jnp.float32),
        in_specs=[hbm] * 5,
        out_specs=pl.BlockSpec(memory_space=pltpu.VMEM),
        scratch_shapes=[
            pltpu.VMEM((kinds, depth, width), jnp.bfloat16),
            pltpu.VMEM((width, depth), jnp.bfloat16),
            pltpu.VMEM((kinds, width, width), jnp.bfloat16),
            pltpu.VMEM((kinds, width, width), jnp.bfloat16),
            parts,
            pltpu.VMEM((kinds, rows + 8, LANES), jnp.float32),
            pltpu.VMEM((kinds, n_row, 24, LANES), jnp.float32),
            pltpu.SMEM((kinds * n_row, 1), jnp.int32),
            pltpu.VMEM((32, LANES), jnp.bfloat16),
            pltpu.VMEM((2, 8, LANES), jnp.float32),
            pair, pair, pair,
            single, single, single,
            pltpu.VMEM((kinds, 2 * rows + 8, LANES), jnp.float32),
            parts, parts,
            pltpu.SMEM(pair_live.shape, jnp.int32),
            pltpu.SMEM(offsets.shape, jnp.int32),
            dma((kinds,)), dma((3,)), dma((kinds + 1,)), dma((4,)), dma((6,)), dma((6,)), dma((2,)),
        ],
        compiler_params=pltpu.CompilerParams(
            collective_id=0, has_side_effects=True, vmem_limit_bytes=60 * 1024 * 1024),
    )(sub_basis, coupling, pair_live, offsets, dual_in.reshape(part_rows, LANES))
    return out.reshape(1, size)


def solution(mesh):
    return jax.shard_map(
        on_device,
        mesh=mesh,
        in_specs=(
            P(("row", "col"), None, None),
            P(("row", "col"), None, None, None),
            P(("row", "col"), None),
            P(("row", "col")),
            P("col", "row"),
        ),
        out_specs=P("col", "row"),
        check_vma=False,
    )
```
